512 devices in a mesh: pipe: 32 (over z, y_hi), expert: 16 (over y_lo, x, core).
Axes of the slice: x: 4, y: 8 (y_hi: 4, y_lo: 2; y = y_hi * 2 + y_lo), z: 8, core: 2. Of those that a mesh axis runs over, the one named last changes fastest.
Arguments:
- tokens: bfloat16 [65536, 2048], P(('pipe', 'expert')), may hold values from -6 to 6
- cotangent: bfloat16 [65536, 2048], P(('pipe', 'expert')), may hold values from -6 to 6
- chosen: int32 [512, 64, 2], P(('pipe', 'expert')), may hold values from 0 to 127, as said below
- gate_value: bfloat16 [512, 64, 2], P(('pipe', 'expert')), may hold values from 0.049804688 to 1
- gate_weight: bfloat16 [2048, 65536], P(None, ('pipe', 'expert')), may hold values from -0.125 to 0.125
- up_weight: bfloat16 [2048, 65536], P(None, ('pipe', 'expert')), may hold values from -0.125 to 0.125
- down_weight: bfloat16 [65536, 2048], P(('pipe', 'expert')), may hold values from -0.1875 to 0.1875
Outputs:
- token_grad: bfloat16 [65536, 2048], P(('pipe', 'expert'))
- gate_grad: float32 [512, 64, 2], P(('pipe', 'expert'))
- gate_weight_grad: bfloat16 [2048, 65536], P(None, ('pipe', 'expert'))
- up_weight_grad: bfloat16 [2048, 65536], P(None, ('pipe', 'expert'))
- down_weight_grad: bfloat16 [65536, 2048], P(('pipe', 'expert'))
The draws below stay inside these ranges and needn't reach their ends.
Inputs may be any that keep to these rules, and one draw needn't show every extreme that they name: `chosen`: for each routing group and expert, the 2 entries are different token indices within that group's 128 tokens.
All inputs are finite; a program needn't handle non-finite values.
Results may differ from the reference program's by a relative error of at most 0.0095.
Values may be sent and summed in bfloat16 or wider, within the bound.
No kernel may reach another device: no remote copies, remote signals or barrier semaphores. Data moves between devices by JAX's collectives and lax.ppermute only.
A program may use at most 128 MiB of HBM per device.

```python
import math
import jax
import jax.numpy as jnp
from jax import lax

D = 2048
H = 1024
TOK_DEV = 128
PICK = 2
BLOCKS = 8
H_DEV = 128
EXPERTS = 64
TOKENS = 65536
DEVICES = 512


def draw_chosen(key, part):
    groups = TOKENS // TOK_DEV
    keys = jax.random.split(key, groups * EXPERTS)

    def pick_some(one_key):
        return jax.random.permutation(one_key, TOK_DEV)[:PICK]
    picked = jax.vmap(pick_some)(keys)
    return picked.reshape(groups, EXPERTS, PICK).astype(jnp.int32)


def block_levels(rng, shape, cuts, low, largest):
    loudness, own = 1.0, jax.random.fold_in(rng, 6)
    for dim, blocks in cuts:
        steps = jnp.exp(jax.random.uniform(jax.random.fold_in(own, dim), (blocks,), jnp.float32, low / len(cuts), largest / len(cuts)))
        loudness = loudness * jnp.repeat(steps, shape[dim] // blocks).reshape([-1 if axis == dim else 1 for axis in range(len(shape))])
    return loudness


def noise(rng, extent, spread, limit, cuts=(), held_as=jnp.bfloat16):
    factor_of = block_levels(rng, extent, cuts, -0.22, 0.18) if cuts else 1.0
    result = jax.random.normal(rng, extent, jnp.float32) * spread * factor_of
    return jnp.minimum(jnp.maximum(result, -limit), limit).astype(held_as)


def setup_inputs(seed: int = 0) -> dict:
    seeds = jax.random.split(jax.random.key(seed), 8)
    return {
        "tokens": noise(seeds[0], (TOKENS, D), 1.0, 6.0, ((0, 512),)),
        "cotangent": noise(seeds[1], (TOKENS, D), 1.0, 6.0, ((0, 512),)),
        "chosen": draw_chosen(jax.random.fold_in(seeds[7], 71), 0),
        "gate_value": jnp.clip(jnp.exp(math.log(1.0) - 2.9996462 * jax.random.uniform(seeds[3], (DEVICES, EXPERTS, PICK), jnp.float32) ** block_levels(seeds[3], (DEVICES, EXPERTS, PICK), ((0, 512),), -0.2, 0.2)), 0.049804688, 1.0).astype(jnp.bfloat16),
        "gate_weight": noise(seeds[4], (D, EXPERTS * H), D ** -0.5, 0.125, ((1, 512),)),
        "up_weight": noise(seeds[5], (D, EXPERTS * H), D ** -0.5, 0.125, ((1, 512),)),
        "down_weight": noise(seeds[6], (EXPERTS * H, D), H ** -0.5, 0.1875, ((0, 512),)),
    }


def reference(tokens, cotangent, chosen, gate_value, gate_weight, up_weight, down_weight):
    groups = TOKENS // TOK_DEV
    offsets = (jnp.arange(groups, dtype=jnp.int32) * TOK_DEV)[:, None]
    gate_blocks = jnp.transpose(gate_weight.reshape(D, EXPERTS, H), (1, 0, 2))
    up_blocks = jnp.transpose(up_weight.reshape(D, EXPERTS, H), (1, 0, 2))
    down_blocks = down_weight.reshape(EXPERTS, H, D)
    lists = jnp.transpose(chosen, (1, 0, 2))
    gates = jnp.transpose(gate_value, (1, 0, 2))
    contract_rows = (((0,), (0,)), ((), ()))

    def one_expert(carry, inputs):
        picks_here, gate_here, w_gate, w_up, w_down = inputs
        slot_rows = (picks_here.astype(jnp.int32) + offsets).reshape(-1).astype(jnp.int32)
        picked = tokens[slot_rows]
        dpicked = cotangent[slot_rows]
        factor = gate_here.reshape(-1).astype(jnp.float32)[:, None]
        gate_pre = jnp.dot(picked, w_gate, preferred_element_type=jnp.float32)
        up_pre = jnp.dot(picked, w_up, preferred_element_type=jnp.float32)
        back = jnp.dot(dpicked, w_down.T, preferred_element_type=jnp.float32)
        logistic = jax.nn.sigmoid(gate_pre)
        activated = gate_pre * logistic
        hidden = (activated * up_pre).astype(jnp.bfloat16)
        router = jnp.sum(hidden.astype(jnp.float32) * back, axis=1)
        hidden_grad = factor * back
        gate_pre_grad = (hidden_grad * up_pre * logistic * (1.0 + gate_pre * (1.0 - logistic))).astype(jnp.bfloat16)
        up_pre_grad = (hidden_grad * activated).astype(jnp.bfloat16)
        scaled = (factor * dpicked.astype(jnp.float32)).astype(jnp.bfloat16)
        down_grad = lax.dot_general(hidden, scaled, contract_rows, preferred_element_type=jnp.float32).astype(jnp.bfloat16)
        gate_grad_w = lax.dot_general(picked, gate_pre_grad, contract_rows, preferred_element_type=jnp.float32).astype(jnp.bfloat16)
        up_grad_w = lax.dot_general(picked, up_pre_grad, contract_rows, preferred_element_type=jnp.float32).astype(jnp.bfloat16)
        slot_count = slot_rows.shape[0]
        gate_pieces = gate_pre_grad.astype(jnp.float32).reshape(slot_count, BLOCKS, H_DEV)
        up_pieces = up_pre_grad.astype(jnp.float32).reshape(slot_count, BLOCKS, H_DEV)
        wg_pieces = w_gate.astype(jnp.float32).reshape(D, BLOCKS, H_DEV)
        wu_pieces = w_up.astype(jnp.float32).reshape(D, BLOCKS, H_DEV)
        block_grad = jnp.einsum("rbk,dbk->rbd", gate_pieces, wg_pieces, precision=lax.Precision.HIGHEST)
        block_grad = block_grad + jnp.einsum("rbk,dbk->rbd", up_pieces, wu_pieces, precision=lax.Precision.HIGHEST)
        rounded = lax.optimization_barrier(block_grad.astype(jnp.bfloat16))
        summed = jnp.sum(rounded.astype(jnp.float32), axis=1)
        carry = carry.at[slot_rows].add(summed)
        return carry, (router, gate_grad_w, up_grad_w, down_grad)

    start = jnp.zeros((TOKENS, D), jnp.float32)
    total_grad, outputs = lax.scan(one_expert, start, (lists, gates, gate_blocks, up_blocks, down_blocks))
    routers, gate_grads, up_grads, down_grads = outputs
    token_grad = total_grad.astype(jnp.bfloat16)
    gate_grad = jnp.transpose(routers.reshape(EXPERTS, groups, PICK), (1, 0, 2))
    gate_weight_grad = jnp.transpose(gate_grads, (1, 0, 2)).reshape(D, EXPERTS * H)
    up_weight_grad = jnp.transpose(up_grads, (1, 0, 2)).reshape(D, EXPERTS * H)
    down_weight_grad = down_grads.reshape(EXPERTS * H, D)
    return token_grad, gate_grad, gate_weight_grad, up_weight_grad, down_weight_grad
```

```python
import jax
import jax.numpy as jnp
from jax import lax
from jax.experimental import pallas as pl
from jax.experimental.pallas import tpu as pltpu
from jax.sharding import Mesh, PartitionSpec as P

AXES = ("z", "yh", "yl", "x", "c")
ZY = ("z", "yh", "yl")
F32 = jnp.float32
BF16 = jnp.bfloat16
PAD = 128


CONTRACT_ROWS = (((0,), (0,)), ((), ()))
CONTRACT_LAST = (((1,), (1,)), ((), ()))


def call(body, out_shape, name):
    return pl.pallas_call(
        body,
        out_shape=out_shape,
        name=name,
        compiler_params=pltpu.CompilerParams(vmem_limit_bytes=48 << 20),
    )


def forward_body(*refs):
    pieces, (wg, wu, gate_out, up_out) = refs[:-4], refs[-4:]
    weights = jnp.concatenate([wg[...], wu[...]], axis=1)
    width = wg.shape[1]
    for i, piece in enumerate(pieces):
        n = piece.shape[0]
        pre = jnp.dot(piece[...], weights, preferred_element_type=F32)
        gate_out[i * n : (i + 1) * n, :] = pre[:, :width]
        up_out[i * n : (i + 1) * n, :] = pre[:, width:]


def forward(pieces, wg, wu):
    rows = sum(p.shape[0] for p in pieces)
    shape = jax.ShapeDtypeStruct((rows, wg.shape[1]), F32)
    return call(forward_body, (shape, shape), "forward")(*pieces, wg, wu)


def backward_body(*refs):
    pieces = refs[:-8]
    gate_ref, up_ref, wg, wu, wd, grad_out, hidden_out, both_out = refs[-8:]
    weights = jnp.concatenate([wg[...], wu[...]], axis=1)
    down = wd[...]
    features = wd.shape[1]
    for i, piece in enumerate(pieces):
        n = piece.shape[0]
        span = slice(i * n, (i + 1) * n)
        gate_pre = gate_ref[span, :]
        up_pre = up_ref[span, :]
        hidden_grad = lax.dot_general(piece[...], down, CONTRACT_LAST, preferred_element_type=F32)
        logistic = 1.0 / (1.0 + jnp.exp(-gate_pre))
        activated = gate_pre * logistic
        hidden = (activated * up_pre).astype(BF16)
        router = jnp.sum(hidden.astype(F32) * hidden_grad, axis=1, keepdims=True)
        gate_grad = (
            hidden_grad * up_pre * logistic * (1.0 + gate_pre * (1.0 - logistic))
        ).astype(BF16)
        up_grad = (hidden_grad * activated).astype(BF16)
        both = jnp.concatenate([gate_grad, up_grad], axis=1)
        hidden_out[span, :] = hidden
        both_out[span, :] = both
        grad_out[span, :features] = lax.dot_general(
            both, weights, CONTRACT_LAST, preferred_element_type=F32
        ).astype(BF16)
        grad_out[span, features:] = jnp.broadcast_to(router, (n, PAD)).astype(BF16)


def backward(pieces, gate_pre, up_pre, wg, wu, wd):
    rows, width = gate_pre.shape
    out = (
        jax.ShapeDtypeStruct((rows, wd.shape[1] + PAD), BF16),
        jax.ShapeDtypeStruct((rows, width), BF16),
        jax.ShapeDtypeStruct((rows, 2 * width), BF16),
    )
    return call(backward_body, out, "backward")(*pieces, gate_pre, up_pre, wg, wu, wd)


def weights_body(*refs):
    half = (len(refs) - 7) // 2
    xs, dys = refs[:half], refs[half : 2 * half]
    hid_a, hid_b, both_a, both_b, gate_out, up_out, down_out = refs[2 * half :]
    width = hid_a.shape[1]
    x = jnp.concatenate([r[...] for r in xs], axis=0)
    both = jnp.concatenate([both_a[...], both_b[...]], axis=0)
    pair = lax.dot_general(x, both, CONTRACT_ROWS, preferred_element_type=F32)
    gate_out[...] = pair[:, :width].astype(BF16)
    up_out[...] = pair[:, width:].astype(BF16)
    dy = jnp.concatenate([r[...] for r in dys], axis=0)
    hidden = jnp.concatenate([hid_a[...], hid_b[...]], axis=0)
    down_out[...] = lax.dot_general(
        hidden, dy, CONTRACT_ROWS, preferred_element_type=F32
    ).astype(BF16)


def weight_grads(xs, dys, hid_a, hid_b, both_a, both_b):
    features, width = xs[0].shape[1], hid_a.shape[1]
    out = (
        jax.ShapeDtypeStruct((features, width), BF16),
        jax.ShapeDtypeStruct((features, width), BF16),
        jax.ShapeDtypeStruct((width, features), BF16),
    )
    return call(weights_body, out, "weights")(*xs, *dys, hid_a, hid_b, both_a, both_b)


def add_body(mine, theirs, *outs):
    n = outs[0].shape[0]
    for i, out in enumerate(outs):
        span = slice(i * n, (i + 1) * n)
        out[...] = (mine[span, :].astype(F32) + theirs[span, :].astype(F32)).astype(BF16)


def add_pieces(mine, theirs, count):
    shape = jax.ShapeDtypeStruct((mine.shape[0] // count, mine.shape[1]), BF16)
    return call(add_body, (shape,) * count, "add")(mine, theirs)


def along_x(value, shift):
    size = lax.axis_size("x")
    return lax.ppermute(value, "x", [(i, (i + shift) % size) for i in range(size)])


def swap(value):
    return lax.ppermute(value, "c", [(0, 1), (1, 0)])


def per_device(tokens, cotangent, chosen, gate_value, wg, wu, wd):
    tok, features = tokens.shape
    experts, picks = chosen.shape[1:]
    slots = experts * picks
    listed = chosen[0].reshape(-1)
    factor = gate_value[0].reshape(-1).astype(F32)[:, None]
    onehot = (listed[:, None] == jnp.arange(tok, dtype=jnp.int32)[None, :]).astype(BF16)
    x_rows = jnp.dot(onehot, tokens, preferred_element_type=F32).astype(BF16)
    dy_rows = (factor * jnp.dot(onehot, cotangent, preferred_element_type=F32)).astype(BF16)

    def exchange(rows):
        wide = rows.shape[1]
        got = lax.all_to_all(
            rows.reshape(experts, picks, wide), ZY, split_axis=0, concat_axis=0, tiled=True
        )
        return got.reshape(slots, wide)

    def spread(rows):
        own = [rows, along_x(rows, 1), along_x(rows, -1), along_x(rows, 2)]
        return own, [swap(p) for p in own]

    x_own, x_other = spread(exchange(x_rows))
    dy_own, dy_other = spread(exchange(dy_rows))
    pre_own = forward(x_own, wg, wu)
    pre_other = forward(x_other, wg, wu)
    grad_own, hid_own, both_own = backward(dy_own, *pre_own, wg, wu, wd)
    grad_other, hid_other, both_other = backward(dy_other, *pre_other, wg, wu, wd)
    theirs = swap(grad_other)
    dwg, dwu, dwd = weight_grads(
        x_own + x_other, dy_own + dy_other, hid_own, hid_other, both_own, both_other
    )
    keep, left, right, far = add_pieces(grad_own, theirs, 4)
    parts = (keep, along_x(left, -1), along_x(right, 1), along_x(far, 2))
    total = sum(p.astype(F32) for p in parts).astype(BF16)
    home = exchange(total)
    token_grad = lax.dot_general(
        onehot, home[:, :features], CONTRACT_ROWS, preferred_element_type=F32
    ).astype(BF16)
    gate_grad = (home[:, features : features + 1].astype(F32) / factor).reshape(1, experts, picks)
    return token_grad, gate_grad, dwg, dwu, dwd


def solution(mesh):
    grid = Mesh(mesh.devices.reshape(8, 4, 2, 4, 2), AXES)
    rows, cols = P(AXES, None), P(None, AXES)
    lists = P(AXES, None, None)
    return jax.shard_map(
        per_device,
        mesh=grid,
        in_specs=(rows, rows, lists, lists, cols, cols, rows),
        out_specs=(rows, lists, cols, cols, rows),
        check_vma=False,
    )
```

```python
import functools

import jax
import jax.numpy as jnp
from jax import lax
from jax.experimental import pallas as pl
from jax.experimental.pallas import tpu as pltpu
from jax.sharding import Mesh, PartitionSpec as P

AXES = ("z", "yh", "yl", "x", "c")
ZY = ("z", "yh", "yl")
F32 = jnp.float32
BF16 = jnp.bfloat16
PAD = 128


CONTRACT_ROWS = (((0,), (0,)), ((), ()))
CONTRACT_LAST = (((1,), (1,)), ((), ()))


def call(body, out_shape):
    return pl.pallas_call(
        body, out_shape=out_shape, compiler_params=pltpu.CompilerParams(vmem_limit_bytes=48 << 20)
    )


def forward_body(*refs):
    pieces, (weights, gate_out, up_out) = refs[:-3], refs[-3:]
    half = weights.shape[1] // 2
    for i, piece in enumerate(pieces):
        n = piece.shape[0]
        pre = jnp.dot(piece[...], weights[...], preferred_element_type=F32)
        gate_out[i * n : (i + 1) * n, :] = pre[:, :half]
        up_out[i * n : (i + 1) * n, :] = pre[:, half:]


def forward(pieces, weights):
    rows = sum(p.shape[0] for p in pieces)
    shape = jax.ShapeDtypeStruct((rows, weights.shape[1] // 2), F32)
    return call(forward_body, (shape, shape))(*pieces, weights)


def backward_body(part, *refs):
    count = len(refs) - 7
    pieces = refs[:count]
    gate_ref, up_ref, weights, down, grad_out, hidden_out, both_out = refs[count:]
    features = down.shape[1]
    for i, piece in enumerate(pieces):
        n = piece.shape[0]
        span = slice(i * n, (i + 1) * n)
        source = slice((part + i) * n, (part + i + 1) * n)
        gate_pre = gate_ref[source, :]
        up_pre = up_ref[source, :]
        hidden_grad = lax.dot_general(
            piece[...], down[...], CONTRACT_LAST, preferred_element_type=F32
        )
        logistic = 1.0 / (1.0 + jnp.exp(-gate_pre))
        activated = gate_pre * logistic
        hidden = (activated * up_pre).astype(BF16)
        router = jnp.sum(hidden.astype(F32) * hidden_grad, axis=1, keepdims=True)
        gate_grad = (
            hidden_grad * up_pre * logistic * (1.0 + gate_pre * (1.0 - logistic))
        ).astype(BF16)
        up_grad = (hidden_grad * activated).astype(BF16)
        both = jnp.concatenate([gate_grad, up_grad], axis=1)
        hidden_out[span, :] = hidden
        both_out[span, :] = both
        grad_out[span, :features] = lax.dot_general(
            both, weights[...], CONTRACT_LAST, preferred_element_type=F32
        ).astype(BF16)
        grad_out[span, features:] = jnp.broadcast_to(router, (n, PAD)).astype(BF16)


def backward(pieces, part, pre, weights, down):
    rows = sum(p.shape[0] for p in pieces)
    width, features = down.shape
    out = (
        jax.ShapeDtypeStruct((rows, features + PAD), BF16),
        jax.ShapeDtypeStruct((rows, width), BF16),
        jax.ShapeDtypeStruct((rows, 2 * width), BF16),
    )
    body = functools.partial(backward_body, part)
    return call(body, out)(*pieces, *pre, weights, down)


def weights_body(count, *refs):
    xs, dys = refs[:count], refs[count : 2 * count]
    rest = refs[2 * count :]
    groups = (len(rest) - 4) // 2
    hiddens, boths = rest[:groups], rest[groups : 2 * groups]
    mine_up, mine_down, send_up, send_down = rest[2 * groups :]
    features, width = send_up.shape[0] // 2, send_up.shape[1]
    x = jnp.concatenate([r[...] for r in xs], axis=0)
    both = jnp.concatenate([r[...] for r in boths], axis=0)
    grads = lax.dot_general(x, both, CONTRACT_ROWS, preferred_element_type=F32)
    mine_up[:features, :] = grads[:, :width]
    send_up[:features, :] = grads[:, width : 2 * width].astype(BF16)
    mine_up[features:, :] = grads[:, 2 * width : 3 * width]
    send_up[features:, :] = grads[:, 3 * width :].astype(BF16)
    dy = jnp.concatenate([r[...] for r in dys], axis=0)
    hidden = jnp.concatenate([r[...] for r in hiddens], axis=0)
    down = lax.dot_general(hidden, dy, CONTRACT_ROWS, preferred_element_type=F32)
    mine_down[...] = down[:width, :]
    send_down[...] = down[width:, :].astype(BF16)


def weight_grads(xs, dys, hiddens, boths):
    features, width = xs[0].shape[1], hiddens[0].shape[1] // 2
    out = (
        jax.ShapeDtypeStruct((2 * features, width), F32),
        jax.ShapeDtypeStruct((width, features), F32),
        jax.ShapeDtypeStruct((2 * features, width), BF16),
        jax.ShapeDtypeStruct((width, features), BF16),
    )
    body = functools.partial(weights_body, len(xs))
    return call(body, out)(*xs, *dys, *hiddens, *boths)


def add(a, b):
    return a.astype(F32) + b.astype(F32)


def near(value):
    return lax.ppermute(value, "x", [(i, i ^ 1) for i in range(4)])


def across(value):
    return lax.ppermute(value, "x", [(i, 3 - i) for i in range(4)])


def swap(value):
    return lax.ppermute(value, "c", [(0, 1), (1, 0)])


def exchange(value):
    return lax.all_to_all(value, ZY, split_axis=0, concat_axis=0, tiled=True)


def per_device(tokens, cotangent, chosen, gate_value, wg, wu, wd):
    tok, features = tokens.shape
    experts, picks = chosen.shape[1:]
    slots = experts * picks
    listed = chosen[0].reshape(-1)
    factor = gate_value[0].reshape(-1).astype(F32)[:, None]
    onehot = (listed[:, None] == jnp.arange(tok, dtype=jnp.int32)[None, :]).astype(BF16)
    x_rows = jnp.dot(onehot, tokens, preferred_element_type=F32).astype(BF16)
    dy_rows = (factor * jnp.dot(onehot, cotangent, preferred_element_type=F32)).astype(BF16)
    cut = (experts, picks, features)
    got = exchange(jnp.concatenate([x_rows.reshape(cut), dy_rows.reshape(cut)], axis=1))
    x_own = got[:, :picks].reshape(slots, features)
    dy_own = got[:, picks:].reshape(slots, features)

    wgu_near = near(jnp.concatenate([wg, wu], axis=0))
    down = jnp.concatenate([wd, near(wd)], axis=0)
    weights = jnp.concatenate([wg, wgu_near[:features], wu, wgu_near[features:]], axis=1)

    x_far, dy_far = across(x_own), across(dy_own)
    x_other, dy_other = swap(x_own), swap(dy_own)
    x_cross, dy_cross = swap(x_far), swap(dy_far)

    pre = forward([x_own, x_other], weights)
    grad, hid_a, both_a = backward([dy_own, dy_other], 0, pre, weights, down)
    keep = add(grad[:slots], swap(grad[slots:]))
    pre = forward([x_far, x_cross], weights)
    grad_cross, hid_c, both_c = backward([dy_cross], 1, pre, weights, down)
    theirs = swap(grad_cross)
    grad_far, hid_b, both_b = backward([dy_far], 0, pre, weights, down)
    arrived = across(add(grad_far, theirs).astype(BF16))
    total = add(keep, arrived).astype(BF16)
    home = exchange(total.reshape(experts, picks, -1)).reshape(slots, -1)

    mine_up, mine_down, send_up, send_down = weight_grads(
        [x_own, x_other, x_far, x_cross],
        [dy_own, dy_other, dy_far, dy_cross],
        [hid_a, hid_b, hid_c],
        [both_a, both_b, both_c],
    )
    up = near(send_up)
    dwg = add(mine_up[:features], up[:features]).astype(BF16)
    dwu = add(mine_up[features:], up[features:]).astype(BF16)
    dwd = add(mine_down, near(send_down)).astype(BF16)
    token_grad = lax.dot_general(
        onehot, home[:, :features], CONTRACT_ROWS, preferred_element_type=F32
    ).astype(BF16)
    gate_grad = (home[:, features : features + 1].astype(F32) / factor).reshape(1, experts, picks)
    return token_grad, gate_grad, dwg, dwu, dwd


def solution(mesh):
    grid = Mesh(mesh.devices.reshape(8, 4, 2, 4, 2), AXES)
    rows, cols = P(AXES, None), P(None, AXES)
    lists = P(AXES, None, None)
    return jax.shard_map(
        per_device,
        mesh=grid,
        in_specs=(rows, rows, lists, lists, cols, cols, rows),
        out_specs=(rows, lists, cols, cols, rows),
        check_vma=False,
    )
```

```python
import functools

import jax
import jax.numpy as jnp
from jax import lax
from jax.experimental import pallas as pl
from jax.experimental.pallas import tpu as pltpu
from jax.sharding import Mesh, PartitionSpec as P

AXES = ("z", "yh", "yl", "x", "c")
ZY = ("z", "yh", "yl")
F32 = jnp.float32
BF16 = jnp.bfloat16
PAD = 128


CONTRACT_ROWS = (((0,), (0,)), ((), ()))
CONTRACT_LAST = (((1,), (1,)), ((), ()))


def call(body, out_shape):
    return pl.pallas_call(
        body, out_shape=out_shape, compiler_params=pltpu.CompilerParams(vmem_limit_bytes=48 << 20)
    )


def joined_up(wg, wu, packed):
    n = wg.shape[0]
    return jnp.concatenate([wg[...], packed[:n, :], wu[...], packed[n : 2 * n, :]], axis=1)


def forward_pieces(pieces, weights, gate_out, up_out):
    half = weights.shape[1] // 2
    for i, piece in enumerate(pieces):
        n = piece.shape[0]
        pre = jnp.dot(piece[...], weights[...], preferred_element_type=F32)
        gate_out[i * n : (i + 1) * n, :] = pre[:, :half]
        up_out[i * n : (i + 1) * n, :] = pre[:, half:]


def forward_body(*refs):
    forward_pieces(refs[:-3], *refs[-3:])


def forward_join_body(*refs):
    pieces, (wg, wu, packed, gate_out, up_out, weights) = refs[:-6], refs[-6:]
    weights[...] = joined_up(wg, wu, packed)
    forward_pieces(pieces, weights, gate_out, up_out)


def forward(pieces, weights):
    rows = sum(p.shape[0] for p in pieces)
    shape = jax.ShapeDtypeStruct((rows, weights.shape[1] // 2), F32)
    return call(forward_body, (shape, shape))(*pieces, weights)


def forward_join(pieces, wg, wu, packed):
    rows = sum(p.shape[0] for p in pieces)
    features, width = wg.shape
    shape = jax.ShapeDtypeStruct((rows, 2 * width), F32)
    joined = jax.ShapeDtypeStruct((features, 4 * width), BF16)
    return call(forward_join_body, (shape, shape, joined))(
        *pieces, wg, wu, packed
    )


def backward_pieces(part, pieces, gate_ref, up_ref, weights, down, grad_out, hidden_out, both_out):
    features = down.shape[1]
    for i, piece in enumerate(pieces):
        n = piece.shape[0]
        span = slice(i * n, (i + 1) * n)
        source = slice((part + i) * n, (part + i + 1) * n)
        gate_pre = gate_ref[source, :]
        up_pre = up_ref[source, :]
        hidden_grad = lax.dot_general(
            piece[...], down[...], CONTRACT_LAST, preferred_element_type=F32
        )
        logistic = 1.0 / (1.0 + jnp.exp(-gate_pre))
        activated = gate_pre * logistic
        hidden = (activated * up_pre).astype(BF16)
        router = jnp.sum(hidden.astype(F32) * hidden_grad, axis=1, keepdims=True)
        gate_grad = (
            hidden_grad * up_pre * logistic * (1.0 + gate_pre * (1.0 - logistic))
        ).astype(BF16)
        up_grad = (hidden_grad * activated).astype(BF16)
        both = jnp.concatenate([gate_grad, up_grad], axis=1)
        hidden_out[span, :] = hidden
        both_out[span, :] = both
        grad = lax.dot_general(both, weights[...], CONTRACT_LAST, preferred_element_type=F32)
        tail = jnp.broadcast_to(router, (n, PAD))
        if isinstance(grad_out, list):
            out, rows = grad_out[i], slice(0, n)
        else:
            out, rows = grad_out, span
        out[rows, :features] = grad.astype(BF16)
        out[rows, features:] = tail.astype(BF16)


def backward_body(part, *refs):
    backward_pieces(part, refs[:-7], *refs[-7:])


def backward_join_body(*refs):
    dy_a, dy_b, gate_ref, up_ref, weights, wd, packed = refs[:7]
    grad_a, grad_b, hidden_out, both_out, down = refs[7:]
    width, features = wd.shape
    down[:width, :] = wd[...]
    for i in range(features // width):
        start = 2 * features + i * width
        down[width:, i * width : (i + 1) * width] = packed[start : start + width, :]
    backward_pieces(
        0, (dy_a, dy_b), gate_ref, up_ref, weights, down, [grad_a, grad_b], hidden_out, both_out
    )


def backward(pieces, part, pre, weights, down):
    rows = sum(p.shape[0] for p in pieces)
    width, features = down.shape
    out = (
        jax.ShapeDtypeStruct((rows, features + PAD), BF16),
        jax.ShapeDtypeStruct((rows, width), BF16),
        jax.ShapeDtypeStruct((rows, 2 * width), BF16),
    )
    body = functools.partial(backward_body, part)
    return call(body, out)(*pieces, *pre, weights, down)


def backward_join(dy_a, dy_b, pre, weights, wd, packed):
    rows, (width, features) = dy_a.shape[0], wd.shape
    grad = jax.ShapeDtypeStruct((rows, features + PAD), BF16)
    out = (
        grad,
        grad,
        jax.ShapeDtypeStruct((2 * rows, 2 * width), BF16),
        jax.ShapeDtypeStruct((2 * rows, 4 * width), BF16),
        jax.ShapeDtypeStruct((2 * width, features), BF16),
    )
    return call(backward_join_body, out)(
        dy_a, dy_b, *pre, weights, wd, packed
    )


def weights_body(count, *refs):
    xs, dys = refs[:count], refs[count : 2 * count]
    rest = refs[2 * count :]
    groups = (len(rest) - 4) // 2
    hiddens, boths = rest[:groups], rest[groups : 2 * groups]
    mine_up, mine_down, send_up, send_down = rest[2 * groups :]
    features, width = send_up.shape[0] // 2, send_up.shape[1]
    x = jnp.concatenate([r[...] for r in xs], axis=0)
    both = jnp.concatenate([r[...] for r in boths], axis=0)
    grads = lax.dot_general(x, both, CONTRACT_ROWS, preferred_element_type=F32)
    mine_up[:features, :] = grads[:, :width]
    send_up[:features, :] = grads[:, width : 2 * width].astype(BF16)
    mine_up[features:, :] = grads[:, 2 * width : 3 * width]
    send_up[features:, :] = grads[:, 3 * width :].astype(BF16)
    dy = jnp.concatenate([r[...] for r in dys], axis=0)
    hidden = jnp.concatenate([r[...] for r in hiddens], axis=0)
    down = lax.dot_general(hidden, dy, CONTRACT_ROWS, preferred_element_type=F32)
    mine_down[...] = down[:width, :]
    send_down[...] = down[width:, :].astype(BF16)


def weight_grads(xs, dys, hiddens, boths):
    features, width = xs[0].shape[1], hiddens[0].shape[1] // 2
    out = (
        jax.ShapeDtypeStruct((2 * features, width), F32),
        jax.ShapeDtypeStruct((width, features), F32),
        jax.ShapeDtypeStruct((2 * features, width), BF16),
        jax.ShapeDtypeStruct((width, features), BF16),
    )
    body = functools.partial(weights_body, len(xs))
    return call(body, out)(*xs, *dys, *hiddens, *boths)


def add(a, b):
    return a.astype(F32) + b.astype(F32)


def near(value):
    return lax.ppermute(value, "x", [(i, i ^ 1) for i in range(4)])


def across(value):
    return lax.ppermute(value, "x", [(i, 3 - i) for i in range(4)])


def swap(value):
    return lax.ppermute(value, "c", [(0, 1), (1, 0)])


def exchange(value):
    return lax.all_to_all(value, ZY, split_axis=0, concat_axis=0, tiled=True)


def per_device(tokens, cotangent, chosen, gate_value, wg, wu, wd):
    tok, features = tokens.shape
    experts, picks = chosen.shape[1:]
    slots = experts * picks
    listed = chosen[0].reshape(-1)
    factor = gate_value[0].reshape(-1).astype(F32)[:, None]
    onehot = (listed[:, None] == jnp.arange(tok, dtype=jnp.int32)[None, :]).astype(BF16)
    x_rows = jnp.dot(onehot, tokens, preferred_element_type=F32).astype(BF16)
    dy_rows = (factor * jnp.dot(onehot, cotangent, preferred_element_type=F32)).astype(BF16)
    cut = (experts, picks, features)
    got = exchange(jnp.concatenate([x_rows.reshape(cut), dy_rows.reshape(cut)], axis=1))
    x_own = got[:, :picks].reshape(slots, features)
    dy_own = got[:, picks:].reshape(slots, features)

    width = wd.shape[0]
    tiles = jnp.transpose(wd.reshape(width, -1, width), (1, 0, 2)).reshape(-1, width)
    packed = near(jnp.concatenate([wg, wu, tiles], axis=0))

    x_far, dy_far = across(x_own), across(dy_own)
    x_other, dy_other = swap(x_own), swap(dy_own)
    x_cross, dy_cross = swap(x_far), swap(dy_far)

    *pre, weights = forward_join([x_own, x_other], wg, wu, packed)
    grad_own, grad_other, hid_a, both_a, down = backward_join(
        dy_own, dy_other, pre, weights, wd, packed
    )
    keep = add(grad_own, swap(grad_other))
    pre = forward([x_far, x_cross], weights)
    grad_cross, hid_c, both_c = backward([dy_cross], 1, pre, weights, down)
    theirs = swap(grad_cross)
    grad_far, hid_b, both_b = backward([dy_far], 0, pre, weights, down)
    arrived = across(add(grad_far, theirs).astype(BF16))
    total = add(keep, arrived).astype(BF16)
    home = exchange(total.reshape(experts, picks, -1)).reshape(slots, -1)

    mine_up, mine_down, send_up, send_down = weight_grads(
        [x_own, x_other, x_far, x_cross],
        [dy_own, dy_other, dy_far, dy_cross],
        [hid_a, hid_b, hid_c],
        [both_a, both_b, both_c],
    )
    up = near(send_up)
    dwg = add(mine_up[:features], up[:features]).astype(BF16)
    dwu = add(mine_up[features:], up[features:]).astype(BF16)
    dwd = add(mine_down, near(send_down)).astype(BF16)
    token_grad = lax.dot_general(
        onehot, home[:, :features], CONTRACT_ROWS, preferred_element_type=F32
    ).astype(BF16)
    gate_grad = (home[:, features : features + 1].astype(F32) / factor).reshape(1, experts, picks)
    return token_grad, gate_grad, dwg, dwu, dwd


def solution(mesh):
    grid = Mesh(mesh.devices.reshape(8, 4, 2, 4, 2), AXES)
    rows, cols = P(AXES, None), P(None, AXES)
    lists = P(AXES, None, None)
    return jax.shard_map(
        per_device,
        mesh=grid,
        in_specs=(rows, rows, lists, lists, cols, cols, rows),
        out_specs=(rows, lists, cols, cols, rows),
        check_vma=False,
    )
```
